32 devices in a mesh: groups: 2 (over x), ctx: 16 (over z, y, core).
Axes of the slice: x: 2, y: 2, z: 4, core: 2. Of those that a mesh axis runs over, the one named last changes fastest.
Arguments:
- queries: bfloat16 [2048, 4096], P(('groups', 'ctx')), parts along dimension 0, may hold values from -256 to 256
- text_keys: bfloat16 [2048, 512], P(('groups', 'ctx')), parts along dimension 0, may hold values from -4 to 4
- text_values: bfloat16 [2048, 512], P(('groups', 'ctx')), parts along dimension 0, may hold values from -5 to 5
- image_features: bfloat16 [16384, 256], P(('groups', 'ctx')), parts along dimension 0, may hold values from -300 to 300
- kv_weight: bfloat16 [8192, 1024], P('ctx'), may hold values from -0.0625 to 0.0625
- image_grids: int32 [32, 3], P(('groups', 'ctx')), parts along dimension 0, may hold values from 0 to 58, as said below
Outputs:
- attention: bfloat16 [2048, 4096], P(('groups', 'ctx')), parts along dimension 0
- cache_keys: bfloat16 [2048, 512], P(('groups', 'ctx')), parts along dimension 0
- cache_values: bfloat16 [2048, 512], P(('groups', 'ctx')), parts along dimension 0
The draws below stay inside these ranges and needn't reach their ends.
There are 2 independent parts, one for each index of `groups`. The reference program is written for one: setup_inputs(seed, part) draws one part's arguments, and reference() takes and returns one part's arrays. A program takes and returns all parts, laid end to end along the dimension named above; an argument that names none is the same for every part. Nothing has to cross between parts.
Inputs may be any that keep to these rules, and one draw needn't show every extreme that they name: `image_grids`: row b describes the one image of context shard b: offset o, grid rows gh and grid columns gw with 2 <= gh, gw <= 4; its tokens take positions b * 64 + o to b * 64 + o + gh * gw - 1, token k at grid row k // gw and column k % gw; o + gh * gw <= 62; some shard has a 4 x 4 image.
All inputs are finite; a program needn't handle non-finite values.
Results may differ from the reference program's by a relative error of at most 0.0053.
Values may be sent and summed in bfloat16 or wider, within the bound.
No kernel may reach another device: no remote copies, remote signals or barrier semaphores. Data moves between devices by JAX's collectives and lax.ppermute only.
A program may use at most 128 MiB of HBM per device.

```python
import math
import jax
import jax.numpy as jnp
from jax import lax

D = 8192
HEADS = 32
KV_HEADS = 4
HEAD_DIM = 128
GRID = 4
ROWS = 64
CONTEXT = 1024
N_CTX = 16


def image_layout(key):
    base_key = jax.random.fold_in(key, 11)
    tall_key, wide_key, large_key, small_key, offset_key = jax.random.split(base_key, 5)
    grid_tall = jax.random.randint(tall_key, (N_CTX,), 2, GRID + 1, dtype=jnp.int32)
    grid_wide = jax.random.randint(wide_key, (N_CTX,), 2, GRID + 1, dtype=jnp.int32)
    large_shard = jax.random.randint(large_key, (), 0, N_CTX, dtype=jnp.int32)
    small_shard = (large_shard + 1 + jax.random.randint(small_key, (), 0, N_CTX - 1, dtype=jnp.int32)) % N_CTX
    grid_tall = grid_tall.at[large_shard].set(GRID).at[small_shard].set(2)
    grid_wide = grid_wide.at[large_shard].set(GRID).at[small_shard].set(2)
    room_left = ROWS - 2 - grid_tall * grid_wide
    offsets = jax.random.randint(offset_key, (N_CTX,), 0, room_left + 1, dtype=jnp.int32)
    offsets = offsets.at[small_shard].set(room_left[small_shard])
    return (offsets, grid_tall, grid_wide)


def draw_image_grids(key, part):
    offsets, grid_tall, grid_wide = image_layout(key)
    return jnp.stack([offsets, grid_tall, grid_wide], axis=1).astype(jnp.int32)


def base_keys(key):
    noise = jax.random.normal(jax.random.fold_in(key, 21), (ROWS * N_CTX, KV_HEADS * HEAD_DIM), jnp.float32)
    return jnp.clip(noise, -4.0, 4.0)


def draw_text_keys(key, part):
    keys_f32 = base_keys(key)
    return keys_f32.astype(jnp.bfloat16)


def draw_queries(key, part):
    noise = jax.random.normal(jax.random.fold_in(key, 31), (ROWS * N_CTX, HEADS * HEAD_DIM), jnp.float32)
    noise = jnp.clip(noise * 2.5, -10.0, 10.0)
    return noise.astype(jnp.bfloat16)


def draw_image_features(key, part):
    total_slots = GRID * GRID * N_CTX
    feature_key, slot_key, noise_key = jax.random.split(jax.random.fold_in(key, 51), 3)
    ramp = jnp.arange(D, dtype=jnp.float32) / D
    noise = jnp.clip(jax.random.normal(noise_key, (D, total_slots), jnp.float32), -4.0, 4.0)
    feature_scale = jnp.sqrt(1.0 + 2.0 * ramp) * jnp.exp(jax.random.uniform(feature_key, (D,), jnp.float32, -0.6, 0.6))
    slot_scale = 10.0 ** jax.random.uniform(slot_key, (total_slots,), jnp.float32, 0.0, 1.0)
    return (noise * feature_scale[:, None] * slot_scale[None, :]).astype(jnp.bfloat16)


def level_of(key, shape, cuts, least, high):
    level = 1.0
    for axis_at, shards_of in cuts:
        steps = jax.random.uniform(jax.random.fold_in(jax.random.fold_in(key, 6), axis_at), (shards_of,), jnp.float32, least / len(cuts), high / len(cuts))
        level = level * jnp.repeat(jnp.exp(steps), shape[axis_at] // shards_of).reshape((-1,) + (1,) * (len(shape) - 1 - axis_at))
    return level


def scatter_about(rng, dims, deviation, reach, cuts=(), kind=jnp.bfloat16):
    values = deviation * jax.random.normal(rng, dims, jnp.float32)
    if cuts:
        values = values * level_of(rng, dims, cuts, -0.22, 0.18)
    return jnp.clip(values, -reach, reach).astype(kind)


def setup_inputs(seed: int = 0, part: int = 0) -> dict:
    key_of = jax.random.split(jax.random.key(seed), 7)
    own_keys = jax.random.split(jax.random.fold_in(key_of[6], part), 7)
    queries = draw_queries(jax.random.fold_in(jax.random.fold_in(key_of[6], part), 71), part)
    text_keys = draw_text_keys(jax.random.fold_in(jax.random.fold_in(key_of[6], part), 71), part)
    text_values = scatter_about(own_keys[2], (CONTEXT, KV_HEADS * HEAD_DIM), 1.0, 5.0, ((0, 16),))
    image_features = draw_image_features(jax.random.fold_in(jax.random.fold_in(key_of[6], part), 71), part)
    kv_weight = scatter_about(key_of[4], (D, 2 * KV_HEADS * HEAD_DIM), D ** -0.5, 0.0625, ((0, 16),))
    image_grids = draw_image_grids(jax.random.fold_in(jax.random.fold_in(key_of[6], part), 71), part)
    return {"queries": queries, "text_keys": text_keys, "text_values": text_values, "image_features": image_features, "kv_weight": kv_weight, "image_grids": image_grids}


def rope_tables(time_ids, height_ids, width_ids):
    half_dim = HEAD_DIM // 2
    first_bound = HEAD_DIM // 8
    second_bound = first_bound + 3 * HEAD_DIM // 16
    pair_index = jnp.arange(half_dim, dtype=jnp.int32)
    inv_freq = 1000000.0 ** (-(2.0 * pair_index.astype(jnp.float32)) / HEAD_DIM)
    chosen = jnp.where(pair_index[None, :] < first_bound, time_ids[:, None], jnp.where(pair_index[None, :] < second_bound, height_ids[:, None], width_ids[:, None]))
    angles = chosen.astype(jnp.float32) * inv_freq[None, :]
    cosine = jnp.concatenate([jnp.cos(angles), jnp.cos(angles)], axis=1)
    sine_table = jnp.concatenate([jnp.sin(angles), jnp.sin(angles)], axis=1)
    return (cosine, sine_table)

def rotate(key_heads, cosine, sine_table):
    half_dim = HEAD_DIM // 2
    turned = jnp.concatenate([-key_heads[..., half_dim:], key_heads[..., :half_dim]], axis=-1)
    return key_heads * cosine[:, None, :] + turned * sine_table[:, None, :]

def attend(queries, cache_keys, cache_values):
    length = queries.shape[0]
    head_group = HEADS // KV_HEADS
    block_size = math.gcd(length, 256)
    keys_all = cache_keys.astype(jnp.float32).reshape(length, KV_HEADS, HEAD_DIM)
    values_all = cache_values.astype(jnp.float32).reshape(length, KV_HEADS, HEAD_DIM)
    results = []
    for begin_row in range(0, length, block_size):
        end_row = begin_row + block_size
        query_block = queries[begin_row:end_row].astype(jnp.float32).reshape(block_size, KV_HEADS, head_group, HEAD_DIM)
        scores = jnp.einsum('qgmd,kgd->gmqk', query_block, keys_all[:end_row]) / math.sqrt(HEAD_DIM)
        query_pos = begin_row + jnp.arange(block_size, dtype=jnp.int32)
        key_pos = jnp.arange(end_row, dtype=jnp.int32)
        allowed = key_pos[None, :] <= query_pos[:, None]
        scores = jnp.where(allowed, scores, -1e+30)
        largest = lax.optimization_barrier(jnp.max(scores, axis=-1, keepdims=True))
        weights = jnp.where(allowed, jnp.exp(scores - largest), 0.0)
        totals = lax.optimization_barrier(jnp.sum(weights, axis=-1))
        rounded = lax.optimization_barrier(weights.astype(jnp.bfloat16)).astype(jnp.float32)
        blended = jnp.einsum('gmqk,kgd->qgmd', rounded, values_all[:end_row])
        blended = blended / jnp.transpose(totals, (2, 0, 1))[..., None]
        results.append(blended.reshape(block_size, HEADS * HEAD_DIM).astype(jnp.bfloat16))
    return jnp.concatenate(results, axis=0)

def reference(queries, text_keys, text_values, image_features, kv_weight, image_grids):
    kv_width = KV_HEADS * HEAD_DIM
    slot_count = GRID * GRID
    total_slots = slot_count * N_CTX
    raw_kv = jnp.dot(image_features.T, kv_weight, preferred_element_type=jnp.float32)
    feature_f32 = image_features.astype(jnp.float32)
    power = lax.optimization_barrier(jnp.sum(feature_f32 * feature_f32, axis=0)) / D
    normed = raw_kv * lax.rsqrt(power + 1e-06)[:, None]
    slot_index = jnp.arange(total_slots, dtype=jnp.int32)
    shard_index = slot_index // slot_count
    within = slot_index % slot_count
    grid_rows = image_grids[shard_index]
    offsets = grid_rows[:, 0]
    grid_tall = grid_rows[:, 1]
    grid_wide = grid_rows[:, 2]
    live_slot = within < grid_tall * grid_wide
    image_start = shard_index * ROWS + offsets
    height_ids = image_start + within // grid_wide
    width_ids = image_start + within % grid_wide
    cosine, sine_table = rope_tables(image_start, height_ids, width_ids)
    key_heads = normed[:, :kv_width].reshape(total_slots, KV_HEADS, HEAD_DIM)
    image_keys = rotate(key_heads, cosine, sine_table).reshape(total_slots, kv_width).astype(jnp.bfloat16)
    image_values = normed[:, kv_width:].astype(jnp.bfloat16)
    length = ROWS * N_CTX
    places = jnp.where(live_slot, image_start + within, length).astype(jnp.int32)
    cache_keys = text_keys.at[places].set(image_keys, mode='drop')
    cache_values = text_values.at[places].set(image_values, mode='drop')
    attention = attend(queries, cache_keys, cache_values)
    return (attention, cache_keys, cache_values)
```

```python
import functools
import math

import jax
import jax.numpy as jnp
from jax import lax
from jax.experimental import pallas as pl
from jax.experimental.pallas import tpu as pltpu
from jax.sharding import PartitionSpec as P

HEAD_DIM = 128
GRID = 4
SLOTS = GRID * GRID
TAIL = 128
NEG = -1e30


def rope_tables(time_ids, height_ids, width_ids):
    half_dim = HEAD_DIM // 2
    first_bound = HEAD_DIM // 8
    second_bound = first_bound + 3 * HEAD_DIM // 16
    pair_index = jnp.arange(half_dim, dtype=jnp.int32)
    inv_freq = 1000000.0 ** (-(2.0 * pair_index.astype(jnp.float32)) / HEAD_DIM)
    chosen = jnp.where(
        pair_index[None, :] < first_bound,
        time_ids[:, None],
        jnp.where(pair_index[None, :] < second_bound, height_ids[:, None], width_ids[:, None]),
    )
    angles = chosen.astype(jnp.float32) * inv_freq[None, :]
    cosine = jnp.concatenate([jnp.cos(angles), jnp.cos(angles)], axis=1)
    sine_table = jnp.concatenate([jnp.sin(angles), jnp.sin(angles)], axis=1)
    return (cosine, sine_table)


def rotate(key_heads, cosine, sine_table):
    half_dim = HEAD_DIM // 2
    turned = jnp.concatenate([-key_heads[..., half_dim:], key_heads[..., :half_dim]], axis=-1)
    return key_heads * cosine[:, None, :] + turned * sine_table[:, None, :]


def attend_kernel(text_xors, image_order, rows, me_ref, q_ref, *refs):
    text_refs = refs[: len(text_xors)]
    image_refs = refs[len(text_xors) : len(text_xors) + len(image_order)]
    own_ref, out_ref, meta_ref = refs[len(text_xors) + len(image_order) :]
    me = me_ref[0]
    width = own_ref.shape[1] // 2
    kv_count = width // HEAD_DIM
    group = q_ref.shape[1] // width
    lane = lax.broadcasted_iota(jnp.int32, (1, HEAD_DIM), 1)
    biases = []
    for ref, xors in zip(text_refs, text_xors):
        lines = []
        for at, x in enumerate(xors):
            tile = ref[pl.ds(at * rows + rows - 16, 16), 0 : 2 * HEAD_DIM].astype(jnp.float32)
            line = jnp.where((me ^ x) < me, tile[15:16] * NEG, NEG)
            meta_ref[pl.ds(me ^ x, 1), :] = line
            lines.append(line[:, :HEAD_DIM])
        per = HEAD_DIM // rows
        parts = []
        for first in range(0, len(lines), per):
            part = lines[first]
            for k in range(1, per):
                part = jnp.where(lane >= k * rows, lines[first + k], part)
            parts.append(part)
        biases.append(jnp.concatenate(parts, axis=1))
    quad = me & 3
    blocks = [(z, m) for ms, _ in image_order for m in ms for z in range(meta_ref.shape[0] // 4)]
    parts = []
    per = HEAD_DIM // SLOTS
    for first in range(0, len(blocks), per):
        part = jnp.full((1, HEAD_DIM), NEG, jnp.float32)
        for k, (z, m) in enumerate(blocks[first : first + per]):
            line = meta_ref[pl.ds(z * 4 + (quad ^ m), 1), :][:, HEAD_DIM:]
            part = jnp.where(lane >= k * SLOTS, line, part)
        parts.append(part)
    image_bias = jnp.concatenate(parts, axis=1)
    factor = math.log2(math.e) / math.sqrt(HEAD_DIM)
    contract = (((1,), (1,)), ((), ()))

    def cols(ref, first):
        return ref[:, pl.ds(pl.multiple_of(first, HEAD_DIM), HEAD_DIM)]

    def heads(g, first, count):
        at = [(g * group + first + h) * HEAD_DIM for h in range(count)]
        q = jnp.concatenate([cols(q_ref, a) for a in at], axis=0)
        ks, vs = g * HEAD_DIM, width + g * HEAD_DIM
        keys = [cols(r, ks) for r in text_refs]
        values = [cols(r, vs) for r in text_refs]
        keys.append(jnp.concatenate([cols(r, ks) for r in image_refs], axis=0))
        values.append(jnp.concatenate([cols(r, vs) for r in image_refs], axis=0))
        scores = [
            lax.dot_general(q, k, contract, preferred_element_type=jnp.float32) + b
            for k, b in zip(keys, biases + [image_bias])
        ]
        own = lax.dot_general(q, cols(own_ref, ks), contract, preferred_element_type=jnp.float32)
        causal = (
            lax.broadcasted_iota(jnp.int32, own.shape, 1)
            <= lax.broadcasted_iota(jnp.int32, own.shape, 0) % rows
        )
        own = jnp.where(causal, own, NEG)
        top = jnp.max(own, axis=1, keepdims=True)
        for s in scores:
            top = jnp.maximum(top, jnp.max(s, axis=1, keepdims=True))
        total = jnp.zeros((count * rows, 1), jnp.float32)
        out = jnp.zeros((count * rows, HEAD_DIM), jnp.float32)
        for s, v in zip(scores + [own], values + [cols(own_ref, vs)]):
            w = jnp.exp2((s - top) * factor)
            total = total + jnp.sum(w, axis=1, keepdims=True)
            out = out + jnp.dot(w.astype(jnp.bfloat16), v, preferred_element_type=jnp.float32)
        out = (out / total).astype(jnp.bfloat16)
        for h, a in enumerate(at):
            out_ref[:, pl.ds(pl.multiple_of(a, HEAD_DIM), HEAD_DIM)] = out[
                h * rows : (h + 1) * rows
            ]

    if sum(r.shape[0] for r in text_refs) <= 2048:
        for g in range(kv_count):
            heads(g, 0, group)
    else:
        lax.fori_loop(
            0, kv_count * group, lambda i, c: (heads(i // group, i % group, 1), c)[1], 0
        )


def body(n, queries, text_keys, text_values, image_features, kv_weight, image_grids):
    me = lax.axis_index("ctx")
    rows = queries.shape[0]
    width = text_keys.shape[1]
    kv_count = width // HEAD_DIM
    features = image_features.shape[0] * n
    far = [1 << k for k in range(2, n.bit_length() - 1)]
    levels = n // 4

    def swap(x, mask):
        return lax.ppermute(x, "ctx", [(i, i ^ mask) for i in range(n)])

    offset, tall, wide = image_grids[0, 0], image_grids[0, 1], image_grids[0, 2]
    count = tall * wide
    row = jnp.arange(rows, dtype=jnp.int32)
    text = jnp.concatenate([text_keys, text_values], axis=1)

    lane = jnp.arange(2 * width, dtype=jnp.int32)
    at = lane % rows
    dead_text = ((at > offset) & (at < offset + count)) | (at == rows - 1)
    dead_slot = lane % SLOTS >= count
    meta = jnp.where(lane < HEAD_DIM, dead_text, dead_slot).astype(jnp.bfloat16)
    sent = jnp.where((row == offset)[:, None], text[rows - 1 :], text)
    sent = jnp.where((row == rows - 1)[:, None], meta[None, :], sent)
    near, near_x = sent, [0]
    for mask in far[:-1]:
        near = jnp.concatenate([near, swap(near, mask)], axis=0)
        near_x = near_x + [x ^ mask for x in near_x]
    distant, distant_x = swap(near, far[-1]), [x ^ far[-1] for x in near_x]
    texts, text_xors = [], []
    for block, xors in ((near, near_x), (distant, distant_x)):
        block = jnp.concatenate([block, swap(block, 2)], axis=0)
        xors = xors + [x ^ 2 for x in xors]
        texts += [block, swap(block, 1)]
        text_xors += [xors, [x ^ 1 for x in xors]]

    partial = lax.dot_general(
        image_features, kv_weight, (((0,), (0,)), ((), ())), preferred_element_type=jnp.float32
    )
    f32 = image_features.astype(jnp.float32)
    squares = jnp.sum(f32 * f32, axis=0)
    tail_lane = jnp.arange(TAIL, dtype=jnp.int32)
    slot = jnp.arange(n * SLOTS, dtype=jnp.int32)
    grid_line = jnp.where(tail_lane == 1, offset, jnp.where(tail_lane == 2, wide, 0))
    tail = jnp.where(
        (tail_lane == 0)[None, :],
        squares[:, None],
        jnp.where((slot // SLOTS == me)[:, None], grid_line[None, :].astype(jnp.float32), 0.0),
    )
    total = jnp.concatenate([partial, tail], axis=1).reshape(levels, 2, 2, SLOTS, -1)
    half = (me & 1, (me >> 1) & 1)
    for mask, axis in ((1, 2), (2, 1)):
        bit = half[mask - 1]
        away = lax.dynamic_index_in_dim(total, 1 - bit, axis, keepdims=False)
        total = lax.dynamic_index_in_dim(total, bit, axis, keepdims=False)
        total = total + swap(away.astype(jnp.bfloat16), mask).astype(jnp.float32)
    total = total.reshape(levels * SLOTS, -1)
    for mask in far:
        total = total + swap(total.astype(jnp.bfloat16), mask).astype(jnp.float32)

    power = total[:, 2 * width] / features
    normed = total[:, : 2 * width] * lax.rsqrt(power + 1e-06)[:, None]
    their = total[:, 2 * width + 1 : 2 * width + 3].astype(jnp.int32)
    local = jnp.arange(levels * SLOTS, dtype=jnp.int32)
    within = local % SLOTS
    start = ((local // SLOTS) * 4 + (me & 3)) * rows + their[:, 0]
    gw = jnp.maximum(their[:, 1], 1)
    cosine, sine_table = rope_tables(start, start + within // gw, start + within % gw)
    key_heads = normed[:, :width].reshape(-1, kv_count, HEAD_DIM)
    image_keys = rotate(key_heads, cosine, sine_table).reshape(-1, width)
    image = jnp.concatenate([image_keys, normed[:, width:]], axis=1).astype(jnp.bfloat16)

    mine = lax.dynamic_slice_in_dim(image, (me >> 2) * SLOTS, SLOTS, 0)
    k = jnp.arange(SLOTS, dtype=jnp.int32)
    one_hot = ((row[:, None] == offset + k[None, :]) & (k < count)[None, :]).astype(jnp.bfloat16)
    placed = jnp.dot(one_hot, mine, preferred_element_type=jnp.float32).astype(jnp.bfloat16)
    image_rows = (row >= offset) & (row < offset + count)
    cache = jnp.where(image_rows[:, None], placed, text)

    image_y = swap(image, 2)
    image_c = swap(jnp.concatenate([image, image_y], axis=0), 1)
    image_order = [([0], None), ([2], None), ([1, 3], None)]
    images = [image, image_y, image_c]
    vmem = pl.BlockSpec(memory_space=pltpu.VMEM)
    attention = pl.pallas_call(
        functools.partial(attend_kernel, text_xors, image_order, rows),
        out_shape=jax.ShapeDtypeStruct(queries.shape, jnp.bfloat16),
        in_specs=[pl.BlockSpec(memory_space=pltpu.SMEM)]
        + [vmem] * (2 + len(texts) + len(images)),
        out_specs=vmem,
        scratch_shapes=[pltpu.VMEM((n, 2 * HEAD_DIM), jnp.float32)],
        name="attend",
        compiler_params=pltpu.CompilerParams(
            vmem_limit_bytes=(20 if n <= 16 else 56) * 1024 * 1024
        ),
        cost_estimate=pl.CostEstimate(
            flops=4 * queries.shape[0] * queries.shape[1] * (n * (rows + SLOTS) + rows),
            bytes_accessed=4 * queries.size + 2 * n * (rows + SLOTS) * 2 * width,
            transcendentals=queries.size // HEAD_DIM * n * (rows + SLOTS),
        ),
    )(me.reshape(1), queries, *texts, *images, cache)
    return (attention, cache[:, :width], cache[:, width:])


def solution(mesh):
    spread = P(("groups", "ctx"), None)
    in_specs = (spread, spread, spread, spread, P("ctx", None), spread)
    return jax.shard_map(
        functools.partial(body, mesh.shape["ctx"]),
        mesh=mesh,
        in_specs=in_specs,
        out_specs=(spread, spread, spread),
        check_vma=False,
    )
```
